32 devices in a mesh: groups: 2 (over x), ctx: 16 (over z, y, core).
Axes of the slice: x: 2, y: 2, z: 4, core: 2. Of those that a mesh axis runs over, the one named last changes fastest.
Arguments:
- features: bfloat16 [64, 16, 24, 192], P(('groups', 'ctx')), parts along dimension 0, may hold values from -6 to 6
- clip_ids: int32 [64], P('groups'), parts along dimension 0, may hold values from 0 to 7, never falling along the last dimension, each value on 1 to 8 neighbouring positions
- gain_first: float32 [192], replicated, may hold values from 0.1 to 1.9
- weight_first: bfloat16 [27, 192, 192], P(None, None, 'ctx'), may hold values from -0.078125 to 0.078125
- gain_second: float32 [192], replicated, may hold values from 0.1 to 1.9
- weight_second: bfloat16 [27, 192, 192], P(None, None, 'ctx'), may hold values from -0.078125 to 0.078125
- gain_third: float32 [192], replicated, may hold values from 0.1 to 1.9
- weight_out: bfloat16 [27, 192, 16], replicated, may hold values from -0.078125 to 0.078125
- embed_weight: bfloat16 [64, 3072], replicated, may hold values from -0.75 to 0.75
- shift_mod: float32 [3072], replicated, may hold values from -3 to 3
- scale_mod: float32 [3072], replicated, may hold values from -0.5 to 0.5
- token_order: int32 [6144], P(('groups', 'ctx')), parts along dimension 0, may hold values from 0 to 3071, each once
Outputs:
- tokens_out: bfloat16 [6144, 3072], P(('groups', 'ctx')), parts along dimension 0
The draws below stay inside these ranges and needn't reach their ends.
There are 2 independent parts, one for each index of `groups`. The reference program is written for one: setup_inputs(seed, part) draws one part's arguments, and reference() takes and returns one part's arrays. A program takes and returns all parts, laid end to end along the dimension named above; an argument that names none is the same for every part. Nothing has to cross between parts.
Inputs may be any that keep to these rules, and one draw needn't show every extreme that they name: `clip_ids`: clip ids never fall along the frames and start at 0; each clip spans 1 to 8 frames, and some clip spans exactly 8. `token_order`: each patch index appears exactly once.
All inputs are finite; a program needn't handle non-finite values.
Results may differ from the reference program's by a relative error of at most 0.014.
Values may be sent and summed in bfloat16 or wider, within the bound.
A program may use at most 128 MiB of HBM per device.

```python
import math
import jax
import jax.numpy as jnp
import numpy as np
from jax import lax

C = 192
CZ = 16
D = 3072
HB = 16
WB = 24
FRAMES = 32
TOKENS = 3072


def block_scale(own_key, extent, pieces, smallest, high):
    gain, own = 1.0, jax.random.fold_in(own_key, 6)
    for dim, shards_of in pieces:
        draws = jnp.exp(jax.random.uniform(jax.random.fold_in(own, dim), (shards_of,), jnp.float32, smallest / len(pieces), high / len(pieces)))
        gain = gain * jnp.repeat(draws, extent[dim] // shards_of).reshape([-1 if axis == dim else 1 for axis in range(len(extent))])
    return gain


def length_profile(count, total, reach, skew):
    loads = [(1 << 20) // math.isqrt(standing ** skew) + 1 for standing in range(2, count + 1)]
    spare, counts = total - reach - (count - 1), [1] * (count - 1)
    while spare > 0:
        candidates = [i for i in range(count - 1) if counts[i] < reach]
        whole, budget = sum([loads[i] for i in candidates]), spare
        for i in candidates:
            extra = min(reach - counts[i], max(1, budget * loads[i] // whole), spare)
            counts[i] = counts[i] + extra
            spare = spare - extra
    return np.array([reach] + counts)


def uneven(own_key, amount, total, bound, slope):
    if amount == 2:
        one = jax.random.randint(own_key, (), max(1, total - bound), min(bound, total - 1) + 1)
        return jnp.stack([one, total - one])
    lengths = jnp.asarray(length_profile(amount, total, bound, slope), jnp.int32)
    couples = (amount - 1) // 2
    donor, taker = lengths[1:1 + 2 * couples:2], lengths[2:2 + 2 * couples:2]
    room = jnp.minimum(donor - 1, bound - taker)
    moved = jax.random.randint(jax.random.fold_in(own_key, 1), (couples,), 0, 1 << 20) % (room + 1)
    lengths = lengths.at[1:1 + 2 * couples:2].set(donor - moved).at[2:2 + 2 * couples:2].set(taker + moved)
    return lengths[jax.random.permutation(jax.random.fold_in(own_key, 2), amount)]


def normal_values(rng, dims, scale, bound, cuts=(), held_as=jnp.bfloat16):
    level = block_scale(rng, dims, cuts, -0.22, 0.18) if cuts else 1.0
    entries = jax.random.normal(rng, dims, jnp.float32) * scale * level
    return jnp.minimum(jnp.maximum(entries, -bound), bound).astype(held_as)


def setup_inputs(seed: int = 0, part: int = 0) -> dict:
    keys = jax.random.split(jax.random.key(seed), 13)
    own_keys = jax.random.split(jax.random.fold_in(keys[12], part), 13)
    return {
        "features": normal_values(own_keys[0], (FRAMES, HB, WB, C), 1.0, 6.0, ((0, 16),)),
        "clip_ids": jnp.searchsorted(jnp.cumsum(uneven(own_keys[1], FRAMES // 4, FRAMES, 8, 2)), jnp.arange(FRAMES), side="right").astype(jnp.int32),
        "gain_first": jnp.clip(1.0 + 0.18 * jax.random.normal(keys[2], (C,), jnp.float32), 0.1, 1.9),
        "weight_first": normal_values(keys[3], (27, C, C), (27 * C) ** -0.5, 0.078125, ((2, 16),)),
        "gain_second": jnp.clip(1.0 + 0.18 * jax.random.normal(keys[4], (C,), jnp.float32), 0.1, 1.9),
        "weight_second": normal_values(keys[5], (27, C, C), (27 * C) ** -0.5, 0.078125, ((2, 16),)),
        "gain_third": jnp.clip(1.0 + 0.18 * jax.random.normal(keys[6], (C,), jnp.float32), 0.1, 1.9),
        "weight_out": normal_values(keys[7], (27, C, CZ), (27 * C) ** -0.5, 0.078125),
        "embed_weight": normal_values(keys[8], (4 * CZ, D), (4 * CZ) ** -0.5, 0.75),
        "shift_mod": normal_values(keys[9], (D,), 0.5, 3.0, (), jnp.float32),
        "scale_mod": jnp.clip(jax.random.uniform(keys[10], (D,), jnp.float32, -0.5, 0.5), -0.5, 0.5),
        "token_order": jax.random.permutation(own_keys[11], TOKENS).astype(jnp.int32),
    }


def earlier_frames(values, clip_ids, steps_back):
    if steps_back == 0:
        return values
    length = values.shape[0]
    moved_back = jnp.concatenate([jnp.zeros((steps_back,) + values.shape[1:], values.dtype), values[:length - steps_back]], axis=0)
    moved_ids = jnp.concatenate([jnp.full((steps_back,), -1, jnp.int32), clip_ids[:length - steps_back].astype(jnp.int32)])
    same_clip = moved_ids == clip_ids.astype(jnp.int32)
    return jnp.where(same_clip[:, None, None, None], moved_back, jnp.zeros((), values.dtype))

def causal_conv(values, clip_ids, weight):
    frames, height, breadth, channels = values.shape
    summed = jnp.zeros((frames * height * breadth, weight.shape[2]), jnp.float32)
    for frame_tap in range(3):
        source = earlier_frames(values, clip_ids, 2 - frame_tap)
        padded = jnp.pad(source, ((0, 0), (1, 1), (1, 1), (0, 0)))
        for row_tap in range(3):
            for col_tap in range(3):
                shifted = padded[:, row_tap:row_tap + height, col_tap:col_tap + breadth, :].reshape(-1, channels)
                summed = summed + jnp.dot(shifted, weight[frame_tap * 9 + row_tap * 3 + col_tap], preferred_element_type=jnp.float32)
    return summed.reshape(frames, height, breadth, weight.shape[2])

def rms_silu(values, gain_vector):
    values = values.astype(jnp.float32)
    normed = values * lax.rsqrt(lax.optimization_barrier(jnp.mean(values * values, axis=-1, keepdims=True)) + 1e-06) * gain_vector.astype(jnp.float32)
    return jax.nn.silu(normed).astype(jnp.bfloat16)

def to_patches(latents):
    frames, height, breadth, latent_depth = latents.shape
    grid = latents.reshape(frames, height // 2, 2, breadth // 2, 2, latent_depth).transpose(0, 1, 3, 2, 4, 5)
    return grid.reshape(frames * (height // 2) * (breadth // 2), 4 * latent_depth)

def modulate(ordered, embed_weight, shift_mod, scale_mod):
    embedded = jnp.dot(ordered, embed_weight, preferred_element_type=jnp.float32)
    center = lax.optimization_barrier(jnp.mean(embedded, axis=-1, keepdims=True))
    centered = embedded - center
    variance = lax.optimization_barrier(jnp.mean(centered * centered, axis=-1, keepdims=True))
    normed = centered * lax.rsqrt(variance + 1e-06)
    return (normed * (1.0 + scale_mod.astype(jnp.float32)) + shift_mod.astype(jnp.float32)).astype(jnp.bfloat16)

def reference(features, clip_ids, gain_first, weight_first, gain_second, weight_second, gain_third, weight_out, embed_weight, shift_mod, scale_mod, token_order):
    first_in = rms_silu(features, gain_first)
    first_out = causal_conv(first_in, clip_ids, weight_first).astype(jnp.bfloat16)
    second_in = rms_silu(first_out, gain_second)
    block_out = (features.astype(jnp.float32) + causal_conv(second_in, clip_ids, weight_second)).astype(jnp.bfloat16)
    head_in = rms_silu(block_out, gain_third)
    latents = causal_conv(head_in, clip_ids, weight_out).astype(jnp.bfloat16)
    patches = to_patches(latents)
    ordered = patches[token_order.astype(jnp.int32)]
    return modulate(ordered, embed_weight, shift_mod, scale_mod)
```

```python
import functools

import jax
import jax.numpy as jnp
import numpy as np
from jax import lax
from jax.experimental import pallas as pl
from jax.experimental.pallas import tpu as pltpu
from jax.sharding import PartitionSpec as P

MESH = pl.DeviceIdType.MESH
ROWS = 16
EPS = 1e-06


def ring_chip(place, chips):
    half = chips // 2
    return jnp.where(place < half, 2 * place, 2 * (chips - 1 - place) + 1)


def ring_place(chip, chips):
    return jnp.where(chip % 2 == 0, chip // 2, chips - 1 - chip // 2)


def rms_silu(values, gain):
    mean = jnp.sum(values * values, axis=-1, keepdims=True) * (1.0 / values.shape[-1])
    normed = values * lax.rsqrt(mean + EPS) * gain
    return (normed / (1.0 + jnp.exp(-normed))).astype(jnp.bfloat16)


def nt_dot(left, right):
    return lax.dot_general(left, right, (((1,), (1,)), ((), ())), preferred_element_type=jnp.float32)


def block_kernel(
    n, frames, height, breadth,
    clip_ref, features_ref, gain1_ref, gain2_ref, gain3_ref, own1_ref, own2_ref, out_w_ref,
    place_ref, tok_ref, pool_ref, keep_ref,
    ordered_ref,
    gathered, halo, acts, taps, latent, patches, final,
    ring_send, ring_recv, pair_send, pair_recv, local_sem, halo_send, halo_recv,
    patch_send, patch_recv, fwd_send, fwd_recv,
):
    me = lax.axis_index("ctx")
    core, chip = lax.rem(me, 2), lax.div(me, 2)
    chips = n // 2
    place = ring_place(chip, chips)
    partner = me + 1 - 2 * core
    follower = lax.rem(me + 1, n)
    size = height * breadth
    channels = features_ref.shape[1]
    depth = 9 * channels
    lanes = taps.shape[2]

    def at(offset):
        return ring_chip(lax.rem(place + offset + chips, chips), chips) * 2 + core

    barrier = pltpu.get_barrier_semaphore()
    for step in range(1, n):
        pl.semaphore_signal(
            barrier, inc=1, device_id={"ctx": lax.rem(me + step, n)}, device_id_type=MESH
        )
    pl.semaphore_wait(barrier, n - 1)

    owns = (own1_ref, own2_ref)

    def ring_copy(w, way, step):
        origin = at(-step) if way == 0 else at(step)
        target = at(1) if way == 0 else at(-1)
        source = owns[w] if step == 0 else gathered.at[w, origin]
        return pltpu.make_async_remote_copy(
            src_ref=source, dst_ref=gathered.at[w, origin],
            send_sem=ring_send.at[w, way, step], recv_sem=ring_recv.at[w, way, step],
            device_id={"ctx": target}, device_id_type=MESH,
        )

    def pair_copy(w, slot, origin):
        source = owns[w] if slot == 0 else gathered.at[w, origin]
        return pltpu.make_async_remote_copy(
            src_ref=source, dst_ref=gathered.at[w, origin],
            send_sem=pair_send.at[w, slot], recv_sem=pair_recv.at[w, slot],
            device_id={"ctx": partner}, device_id_type=MESH,
        )

    reach = (chips // 2, (chips - 1) // 2)

    def begin(w):
        for way in range(2):
            if reach[way] > 0:
                ring_copy(w, way, 0).start()
        pair_copy(w, 0, me).start()

    def advance(w, step):
        for way in range(2):
            if step < reach[way]:
                ring_copy(w, way, step).wait_recv()
                if step + 1 < reach[way]:
                    ring_copy(w, way, step + 1).start()
                origin = at(-step - 1) if way == 0 else at(step + 1)
                pair_copy(w, 1 + 2 * step + way, origin).start()

    def finish(w):
        for way in range(2):
            for step in range(reach[way]):
                ring_copy(w, way, step).wait_send()
        pair_copy(w, 0, me).wait()
        for way in range(2):
            for step in range(reach[way]):
                origin = at(-step - 1) if way == 0 else at(step + 1)
                pair_copy(w, 1 + 2 * step + way, origin).wait()

    def halo_copy(which):
        return pltpu.make_async_remote_copy(
            src_ref=features_ref if which == 0 else acts.at[which - 1],
            dst_ref=halo.at[which],
            send_sem=halo_send.at[which], recv_sem=halo_recv.at[which],
            device_id={"ctx": follower}, device_id_type=MESH,
        )

    halo_copy(0).start()
    begin(0)
    locals_ = [pltpu.make_async_copy(owns[w], gathered.at[w, me], local_sem.at[w]) for w in range(2)]
    for copy in locals_:
        copy.start()

    def kept(tap, frame):
        position = me * frames + frame - 2 + tap
        seen = clip_ref[jnp.maximum(position, 0)]
        same = jnp.logical_and(position >= 0, seen == clip_ref[me * frames + frame])
        return jnp.where(same, 1.0, 0.0)

    columns = lax.broadcasted_iota(jnp.int32, (height, breadth, channels), 1).reshape(size, channels)

    def lay(values, frame_in):
        wide = values.astype(jnp.float32)
        shifted = (
            jnp.where(columns == 0, 0.0, pltpu.roll(wide, 1, 0)),
            wide,
            jnp.where(columns == breadth - 1, 0.0, pltpu.roll(wide, size - 1, 0)),
        )
        for col_tap in range(3):
            for frame in range(frames):
                tap = frame_in - frame
                if 0 <= tap <= 2:
                    piece = shifted[col_tap]
                    if tap < 2:
                        piece = piece * kept(tap, frame)
                    start = (tap * 3 + col_tap) * channels
                    taps[frame, :, start : start + channels] = piece.astype(jnp.bfloat16)

    for frame in range(frames):
        taps[frame, :, depth:] = jnp.zeros((size, lanes - depth), jnp.bfloat16)

    def spread(parts):
        up, mid, down = parts
        zero = jnp.zeros((breadth, mid.shape[1]), jnp.float32)
        return (
            mid
            + jnp.concatenate([zero, up[: size - breadth]], axis=0)
            + jnp.concatenate([down[breadth:], zero], axis=0)
        )

    def conv(frame, weight_of):
        left = taps[frame]
        return spread([nt_dot(left, weight_of(row_tap)) for row_tap in range(3)])

    def gathered_weight(w):
        def weight_of(row_tap):
            part = gathered[w, :, :, row_tap * lanes : (row_tap + 1) * lanes]
            return part.reshape(n * ROWS, lanes)
        return weight_of

    def out_weight(row_tap):
        part = out_w_ref[:, row_tap * lanes : (row_tap + 1) * lanes]
        return jnp.concatenate([part] * 8, axis=0)

    def compact(values):
        return jnp.dot(values, place_ref[...], preferred_element_type=jnp.float32)

    gain1, gain2, gain3 = gain1_ref[...], gain2_ref[...], gain3_ref[...]

    def rows_of(frame):
        return slice(frame * size, (frame + 1) * size)

    for frame in range(frames):
        lay(rms_silu(features_ref[rows_of(frame), :].astype(jnp.float32), gain1), 2 + frame)
    advance(0, 0)
    halo_copy(0).wait()
    for frame in range(2):
        lay(rms_silu(halo[0, rows_of(frame), :].astype(jnp.float32), gain1), frame)
    for step in range(1, reach[0]):
        if step == reach[0] - 1:
            begin(1)
        advance(0, step)
    if reach[0] < 2:
        begin(1)
    for copy in locals_:
        copy.wait()
    finish(0)

    for frame in range(frames):
        first = compact(conv(frame, gathered_weight(0)).astype(jnp.bfloat16))
        acts[0, rows_of(frame), :] = rms_silu(first, gain2)
        if frame < reach[0]:
            advance(1, frame)
    halo_copy(1).start()
    for frame in range(frames):
        lay(acts[0, rows_of(frame), :], 2 + frame)
    for step in range(frames, reach[0] - 1):
        advance(1, step)
    halo_copy(1).wait()
    for frame in range(2):
        lay(halo[1, rows_of(frame), :], frame)
    for step in range(max(frames, reach[0] - 1), reach[0]):
        advance(1, step)
    finish(1)

    for frame in range(frames):
        base = nt_dot(features_ref[rows_of(frame), :], place_ref[...])
        block = compact((base + conv(frame, gathered_weight(1))).astype(jnp.bfloat16))
        acts[1, rows_of(frame), :] = rms_silu(block, gain3)
    halo_copy(2).start()
    for frame in range(frames):
        lay(acts[1, rows_of(frame), :], 2 + frame)
    halo_copy(2).wait()
    for frame in range(2):
        lay(halo[2, rows_of(frame), :], frame)
    for frame in range(frames):
        latent[rows_of(frame), :] = conv(frame, out_weight).astype(jnp.bfloat16) * keep_ref[rows_of(frame), :]
    patches[...] = jnp.dot(
        pool_ref[...], latent[...], preferred_element_type=jnp.float32
    ).astype(jnp.bfloat16)

    def patch_copy(step):
        return pltpu.make_async_remote_copy(
            src_ref=patches, dst_ref=final.at[me],
            send_sem=patch_send.at[step], recv_sem=patch_recv.at[step],
            device_id={"ctx": lax.rem(me + 2 * step, n)}, device_id_type=MESH,
        )

    def forward_copy(step):
        origin = lax.rem(me + n - 2 * step, n)
        return pltpu.make_async_remote_copy(
            src_ref=patches if step == 0 else final.at[origin], dst_ref=final.at[origin],
            send_sem=fwd_send.at[step], recv_sem=fwd_recv.at[step],
            device_id={"ctx": partner}, device_id_type=MESH,
        )

    order = sorted(range(1, chips), key=lambda step: min(step, chips - step))
    for step in reversed(order):
        patch_copy(step).start()
    forward_copy(0).start()
    mine = pltpu.make_async_copy(patches, final.at[me], local_sem.at[2])
    mine.start()
    for step in order:
        patch_copy(step).wait_recv()
        forward_copy(step).start()
    mine.wait()
    for step in order:
        patch_copy(step).wait_send()
    for step in range(chips):
        forward_copy(step).wait()

    packed = final.shape[1]
    count = tok_ref.shape[0]
    device = lax.broadcasted_iota(jnp.int32, (count, packed), 1)
    lane = lax.broadcasted_iota(jnp.int32, (count, final.shape[2]), 1)
    half = final.shape[2] // 2
    tok = tok_ref[...]
    low = jnp.zeros((count, final.shape[2]), jnp.float32)
    high = low
    for owner in range(n):
        rows = final[owner]
        at_low = jnp.where(tok == device + owner * 2 * packed, 1.0, 0.0).astype(jnp.bfloat16)
        at_high = jnp.where(tok == device + (owner * 2 + 1) * packed, 1.0, 0.0).astype(jnp.bfloat16)
        low = low + jnp.dot(at_low, rows, preferred_element_type=jnp.float32)
        high = high + jnp.dot(at_high, rows, preferred_element_type=jnp.float32)
    ordered_ref[...] = jnp.where(lane < half, low, high).astype(jnp.bfloat16)


def modulate_kernel(ordered_ref, embed_ref, shift_ref, scale_ref, out_ref):
    embed = embed_ref[...]
    both = jnp.concatenate([embed, embed], axis=0)
    embedded = jnp.dot(ordered_ref[...], both, preferred_element_type=jnp.float32)
    inverse = 1.0 / embedded.shape[1]
    center = jnp.sum(embedded, axis=-1, keepdims=True) * inverse
    centered = embedded - center
    variance = jnp.sum(centered * centered, axis=-1, keepdims=True) * inverse
    normed = centered * lax.rsqrt(variance + EPS)
    out_ref[...] = (normed * (1.0 + scale_ref[...]) + shift_ref[...]).astype(jnp.bfloat16)


def prepare(weight, lanes, rows):
    channels, outs = weight.shape[1], weight.shape[2]
    split = weight.reshape(3, 3, 3, channels, outs).transpose(4, 1, 0, 2, 3)
    split = split.reshape(outs, 3, 9 * channels)
    padded = jnp.pad(split, ((0, rows - outs), (0, 0), (0, lanes - 9 * channels)))
    return padded.reshape(rows, 3 * lanes)


def body(
    n,
    features, clip_ids, gain_first, weight_first, gain_second, weight_second, gain_third,
    weight_out, embed_weight, shift_mod, scale_mod, token_order,
):
    frames, height, breadth, channels = features.shape
    per, latents = weight_first.shape[2], weight_out.shape[2]
    size = height * breadth
    lanes = -(-9 * channels // 256) * 256
    count = token_order.shape[0]
    width = embed_weight.shape[1]
    patches = frames * size // 4
    packed = patches // 2

    place = np.zeros((n * ROWS, channels), np.float32)
    for channel in range(channels):
        place[channel // per * ROWS + channel % per, channel] = 1
    f, i, j = np.meshgrid(np.arange(frames), np.arange(height), np.arange(breadth), indexing="ij")
    patch = ((f * (height // 2) + i // 2) * (breadth // 2) + j // 2).reshape(-1)
    quarter = (2 * (i % 2) + j % 2).reshape(-1)
    pool = (patch[None, :] % packed == np.arange(packed)[:, None]).astype(np.float32)
    group = np.arange(8 * latents) // latents
    keep = (group[None, :] == (patch // packed * 4 + quarter)[:, None]).astype(np.float32)

    chips = n // 2
    hops = max(1, chips // 2)
    vmem = pl.BlockSpec(memory_space=pltpu.VMEM)
    dma = pltpu.SemaphoreType.DMA
    ordered = pl.pallas_call(
        functools.partial(block_kernel, n, frames, height, breadth),
        out_shape=jax.ShapeDtypeStruct((count, 8 * latents), jnp.bfloat16),
        in_specs=[pl.BlockSpec(memory_space=pltpu.SMEM)] + [vmem] * 11,
        out_specs=vmem,
        scratch_shapes=[
            pltpu.VMEM((2, n, ROWS, 3 * lanes), jnp.bfloat16),
            pltpu.VMEM((3, frames * size, channels), jnp.bfloat16),
            pltpu.VMEM((2, frames * size, channels), jnp.bfloat16),
            pltpu.VMEM((frames, size, lanes), jnp.bfloat16),
            pltpu.VMEM((frames * size, 8 * latents), jnp.bfloat16),
            pltpu.VMEM((packed, 8 * latents), jnp.bfloat16),
            pltpu.VMEM((n, packed, 8 * latents), jnp.bfloat16),
            dma((2, 2, hops)), dma((2, 2, hops)),
            dma((2, 2 * hops + 1)), dma((2, 2 * hops + 1)),
            dma((3,)), dma((3,)), dma((3,)),
            dma((chips,)), dma((chips,)), dma((chips,)), dma((chips,)),
        ],
        compiler_params=pltpu.CompilerParams(
            collective_id=0, has_side_effects=True, vmem_limit_bytes=60 * 1024 * 1024
        ),
        name="block",
    )(
        clip_ids, features.reshape(frames * size, channels),
        gain_first.reshape(1, channels), gain_second.reshape(1, channels),
        gain_third.reshape(1, channels),
        prepare(weight_first, lanes, ROWS), prepare(weight_second, lanes, ROWS),
        prepare(weight_out, lanes, latents),
        jnp.asarray(place, jnp.bfloat16), token_order.reshape(count, 1),
        jnp.asarray(pool, jnp.bfloat16), jnp.asarray(keep, jnp.bfloat16),
    )
    tile = count // 4
    return pl.pallas_call(
        modulate_kernel,
        out_shape=jax.ShapeDtypeStruct((count, width), jnp.bfloat16),
        grid=(count // tile,),
        in_specs=[
            pl.BlockSpec((tile, 8 * latents), lambda step: (step, 0)),
            pl.BlockSpec((embed_weight.shape[0], width), lambda step: (0, 0)),
            pl.BlockSpec((1, width), lambda step: (0, 0)),
            pl.BlockSpec((1, width), lambda step: (0, 0)),
        ],
        out_specs=pl.BlockSpec((tile, width), lambda step: (step, 0)),
        name="modulate",
    )(ordered, embed_weight, shift_mod.reshape(1, width), scale_mod.reshape(1, width))


def solution(mesh):
    in_specs = (
        P(("groups", "ctx"), None, None, None),
        P("groups"),
        P(),
        P(None, None, "ctx"),
        P(),
        P(None, None, "ctx"),
        P(),
        P(),
        P(),
        P(),
        P(),
        P(("groups", "ctx")),
    )
    out_specs = P(("groups", "ctx"), None)
    return jax.shard_map(
        functools.partial(body, mesh.shape["ctx"]),
        mesh=mesh, in_specs=in_specs, out_specs=out_specs, check_vma=False,
    )
```

```python
import functools

import jax
import jax.numpy as jnp
import numpy as np
from jax import lax
from jax.experimental import pallas as pl
from jax.experimental.pallas import tpu as pltpu
from jax.sharding import PartitionSpec as P

MESH = pl.DeviceIdType.MESH
EPS = 1e-06


def ring_chip(place, chips):
    half = chips // 2
    return jnp.where(place < half, 2 * place, 2 * (chips - 1 - place) + 1)


def ring_place(chip, chips):
    return jnp.where(chip % 2 == 0, chip // 2, chips - 1 - chip // 2)


def rms_silu(values, gain):
    mean = jnp.sum(values * values, axis=-1, keepdims=True) * (1.0 / values.shape[-1])
    normed = values * lax.rsqrt(mean + EPS) * gain
    return (normed / (1.0 + jnp.exp(-normed))).astype(jnp.bfloat16)


def nt_dot(left, right):
    return lax.dot_general(left, right, (((1,), (1,)), ((), ())), preferred_element_type=jnp.float32)


def block_kernel(
    n, pairs, per, frames, height, breadth,
    clip_ref, features_ref, gain1_ref, gain2_ref, gain3_ref, own1_ref, own2_ref, out_w_ref,
    place_ref, tok_ref, pool_ref, keep_ref,
    ordered_ref,
    gathered, halo, acts, taps, latent, patches, final,
    ring_send, ring_recv, cross_send, cross_recv, pair_send, pair_recv, local_sem,
    halo_send, halo_recv, patch_send, patch_recv, fwd_send, fwd_recv,
):
    me = lax.axis_index("ctx")
    group = lax.axis_index("groups")
    core, chip = lax.rem(me, 2), lax.div(me, 2)
    parity = lax.rem(group, 2)
    chips = n // 2
    place = ring_place(chip, chips)
    partner = me + 1 - 2 * core
    follower = lax.rem(me + 1, n)
    size = height * breadth
    channels = features_ref.shape[1]
    depth = 9 * channels
    lanes = taps.shape[2]
    rows = gathered.shape[3]
    split = gathered.shape[4] > lanes

    def at(offset):
        return ring_chip(lax.rem(place + offset + chips, chips), chips) * 2 + core

    def rows_of(frame):
        return slice(frame * size, (frame + 1) * size)

    def pack(values, which, frame):
        over = values[:, 128:]
        acts[which, frame, :size, :] = values[:, :128].astype(jnp.bfloat16)
        both = jnp.concatenate([over[: size // 2], over[size // 2 :]], axis=1)
        acts[which, frame, size:, :] = both.astype(jnp.bfloat16)

    def unpack(which, frame):
        both = halo[which, frame, size:, :].astype(jnp.float32)
        over = jnp.concatenate([both[:, : channels - 128], both[:, channels - 128 :]], axis=0)
        return jnp.concatenate([halo[which, frame, :size, :].astype(jnp.float32), over], axis=1)

    for w, own in enumerate((own1_ref, own2_ref)):
        for part in range(3):
            values = own[:, part * lanes : (part + 1) * lanes]
            if split:
                rest = values.astype(jnp.float32)[rows:]
                rest = rest[:, : lanes // 2] + pltpu.roll(rest[:, lanes // 2 :], rows // 2, 0)
                gathered[w, me, part, :, lanes:] = rest.astype(jnp.bfloat16)
            gathered[w, me, part, :, :lanes] = values[:rows]
    for frame in range(frames):
        pack(features_ref[rows_of(frame), :].astype(jnp.float32), 0, frame)

    barrier = pltpu.get_barrier_semaphore()
    for step in range(1, n):
        pl.semaphore_signal(
            barrier, inc=1, device_id={"ctx": lax.rem(me + step, n)}, device_id_type=MESH
        )
    if pairs:
        peer = group + 1 - 2 * parity
        pl.semaphore_signal(barrier, inc=1, device_id={"groups": peer}, device_id_type=MESH)
    pl.semaphore_wait(barrier, n if pairs else n - 1)

    half_way = chips // 2
    if pairs:
        ring_parts = (0, 1 + parity)
        cross_part = 2 - parity
        reach = ((half_way, chips - 1 - half_way), (chips - 1 - half_way, half_way))
    else:
        ring_parts = (0, 1, 2)
        reach = ((half_way, chips - 1 - half_way),) * 3
    hops = ring_send.shape[3]
    last = len(ring_parts) - 1

    def origin_of(way, step):
        return at(-step - 1) if way == 0 else at(step + 1)

    def ring_copy(w, k, way, step):
        block = gathered.at[w, me if step == 0 else origin_of(way, step - 1), ring_parts[k]]
        return pltpu.make_async_remote_copy(
            src_ref=block, dst_ref=block,
            send_sem=ring_send.at[w, k, way, step], recv_sem=ring_recv.at[w, k, way, step],
            device_id={"ctx": at(1) if way == 0 else at(-1)}, device_id_type=MESH,
        )

    def cross_copy(w, way, step, part):
        block = gathered.at[w, origin_of(way, step), part]
        return pltpu.make_async_remote_copy(
            src_ref=block, dst_ref=block,
            send_sem=cross_send.at[w, way, step], recv_sem=cross_recv.at[w, way, step],
            device_id={"groups": peer}, device_id_type=MESH,
        )

    def own_pair(w):
        block = gathered.at[w, me]
        return pltpu.make_async_remote_copy(
            src_ref=block, dst_ref=block,
            send_sem=pair_send.at[w, 0], recv_sem=pair_recv.at[w, 0],
            device_id={"ctx": partner}, device_id_type=MESH,
        )

    def pair_copy(w, k, way, step):
        part = ring_parts[k] if k <= last else cross_part
        block = gathered.at[w, origin_of(way, step), part]
        slot = 1 + (k * 2 + way) * hops + step
        return pltpu.make_async_remote_copy(
            src_ref=block, dst_ref=block,
            send_sem=pair_send.at[w, slot], recv_sem=pair_recv.at[w, slot],
            device_id={"ctx": partner}, device_id_type=MESH,
        )

    def begin(w):
        for k in range(last, -1, -1):
            for way in range(2):
                if reach[k][way] > 0:
                    ring_copy(w, k, way, 0).start()
        own_pair(w).start()

    def arrive(w, step):
        if pairs and step >= 0:
            for way in range(2):
                if step < reach[last][way]:
                    cross_copy(w, way, step, cross_part).wait_recv()
                    pair_copy(w, last + 1, way, step).start()

    def advance(w, step):
        for k in range(last, -1, -1):
            for way in range(2):
                if step < reach[k][way]:
                    ring_copy(w, k, way, step).wait_recv()
                    if step + 1 < reach[k][way]:
                        ring_copy(w, k, way, step + 1).start()
                    if pairs and k == last:
                        cross_copy(w, way, step, ring_parts[k]).start()
                    pair_copy(w, k, way, step).start()
        arrive(w, step - 1)

    def finish(w):
        arrive(w, half_way - 1)
        own_pair(w).wait()
        for k in range(last + 1):
            for way in range(2):
                for step in range(reach[k][way]):
                    ring_copy(w, k, way, step).wait_send()
                    if pairs and k == last:
                        cross_copy(w, way, step, ring_parts[k]).wait_send()
                        pair_copy(w, k + 1, way, step).wait()
                    pair_copy(w, k, way, step).wait()

    def halo_copy(which, frame):
        return pltpu.make_async_remote_copy(
            src_ref=acts.at[which, frame], dst_ref=halo.at[which, frame],
            send_sem=halo_send.at[which, frame], recv_sem=halo_recv.at[which, frame],
            device_id={"ctx": follower}, device_id_type=MESH,
        )

    begin(0)
    for frame in range(frames):
        halo_copy(0, frame).start()

    def kept(tap, frame):
        position = me * frames + frame - 2 + tap
        seen = clip_ref[jnp.maximum(position, 0)]
        same = jnp.logical_and(position >= 0, seen == clip_ref[me * frames + frame])
        return jnp.where(same, 1.0, 0.0)

    columns = lax.broadcasted_iota(jnp.int32, (height, breadth, channels), 1).reshape(size, channels)

    def lay(values, frame_in):
        wide = values.astype(jnp.float32)
        shifted = (
            jnp.where(columns == 0, 0.0, pltpu.roll(wide, 1, 0)),
            wide,
            jnp.where(columns == breadth - 1, 0.0, pltpu.roll(wide, size - 1, 0)),
        )
        for col_tap in range(3):
            for frame in range(frames):
                tap = frame_in - frame
                if 0 <= tap <= 2:
                    piece = shifted[col_tap]
                    if tap < 2:
                        piece = piece * kept(tap, frame)
                    start = (tap * 3 + col_tap) * channels
                    taps[frame, :, start : start + channels] = piece.astype(jnp.bfloat16)

    for frame in range(frames):
        taps[frame, :, depth:] = jnp.zeros((size, lanes - depth), jnp.bfloat16)

    def spread(parts):
        up, mid, down = parts
        zero = jnp.zeros((breadth, mid.shape[1]), jnp.float32)
        return (
            mid
            + jnp.concatenate([zero, up[: size - breadth]], axis=0)
            + jnp.concatenate([down[breadth:], zero], axis=0)
        )

    def conv(frame, w):
        if not split:
            left = taps[frame]
            return spread([
                nt_dot(left, gathered[w, :, part].reshape(n * rows, lanes)) for part in range(3)
            ])
        halves = []
        for half in range(2):
            span = slice(half * lanes // 2, (half + 1) * lanes // 2)
            left = taps[frame, :, span]
            sums = []
            for part in range(3):
                main = gathered[w, :, part, :, span].reshape(n * rows, lanes // 2)
                rest = gathered[w, :, part, :, lanes:].reshape(n * rows, lanes // 2)
                sums.append(nt_dot(left, jnp.concatenate([main, rest], axis=0)))
            halves.append(spread(sums))
        own, other = halves
        edge = n * rows
        moved = pltpu.roll(other[:, edge:], edge - rows // 2, 1)
        return jnp.concatenate([own[:, :edge] + other[:, :edge], own[:, edge:] + moved], axis=1)

    def out_weight(row_tap):
        part = out_w_ref[:, row_tap * lanes : (row_tap + 1) * lanes]
        return jnp.concatenate([part] * 8, axis=0)

    def compact(values):
        return jnp.dot(values, place_ref[...], preferred_element_type=jnp.float32)

    gain1, gain2, gain3 = gain1_ref[...], gain2_ref[...], gain3_ref[...]

    for frame in range(frames):
        lay(rms_silu(features_ref[rows_of(frame), :].astype(jnp.float32), gain1), 2 + frame)
    advance(0, 0)
    for frame in range(frames):
        halo_copy(0, frame).wait()
        lay(rms_silu(unpack(0, frame), gain1), frame)
    for step in range(1, half_way):
        advance(0, step)
        if step == half_way - 2:
            begin(1)
    if half_way < 3:
        begin(1)
    finish(0)

    own = []
    for frame in range(frames):
        first = compact(conv(frame, 0).astype(jnp.bfloat16))
        value = rms_silu(first, gain2)
        pack(value.astype(jnp.float32), 1, frame)
        halo_copy(1, frame).start()
        if frame < half_way:
            advance(1, frame)
        own.append(value)
    for frame in range(frames):
        lay(own[frame], 2 + frame)
    for step in range(frames, half_way):
        advance(1, step)
    for frame in range(frames):
        halo_copy(1, frame).wait()
        lay(unpack(1, frame), frame)
    finish(1)

    own = []
    for frame in range(frames):
        base = nt_dot(features_ref[rows_of(frame), :], place_ref[...])
        block = compact((base + conv(frame, 1)).astype(jnp.bfloat16))
        value = rms_silu(block, gain3)
        pack(value.astype(jnp.float32), 2, frame)
        halo_copy(2, frame).start()
        own.append(value)
    for frame in range(frames):
        lay(own[frame], 2 + frame)
    for frame in range(frames):
        halo_copy(2, frame).wait()
        lay(unpack(2, frame), frame)
    for frame in range(frames):
        left = taps[frame]
        sums = spread([nt_dot(left, out_weight(part)) for part in range(3)])
        latent[rows_of(frame), :] = sums.astype(jnp.bfloat16) * keep_ref[rows_of(frame), :]
    patches[...] = jnp.dot(
        pool_ref[...], latent[...], preferred_element_type=jnp.float32
    ).astype(jnp.bfloat16)

    def patch_copy(step):
        return pltpu.make_async_remote_copy(
            src_ref=patches, dst_ref=final.at[me],
            send_sem=patch_send.at[step], recv_sem=patch_recv.at[step],
            device_id={"ctx": lax.rem(me + 2 * step, n)}, device_id_type=MESH,
        )

    def forward_copy(step):
        origin = lax.rem(me + n - 2 * step, n)
        return pltpu.make_async_remote_copy(
            src_ref=patches if step == 0 else final.at[origin], dst_ref=final.at[origin],
            send_sem=fwd_send.at[step], recv_sem=fwd_recv.at[step],
            device_id={"ctx": partner}, device_id_type=MESH,
        )

    order = sorted(range(1, chips), key=lambda step: min(step, chips - step))
    for step in reversed(order):
        patch_copy(step).start()
    forward_copy(0).start()
    mine = pltpu.make_async_copy(patches, final.at[me], local_sem.at[0])
    mine.start()
    for step in order:
        patch_copy(step).wait_recv()
        forward_copy(step).start()
    mine.wait()
    for step in order:
        patch_copy(step).wait_send()
    for step in range(chips):
        forward_copy(step).wait()

    packed, packed_lanes = final.shape[1], final.shape[2]
    count = tok_ref.shape[1]
    device = lax.broadcasted_iota(jnp.int32, (count, packed), 1)
    lane = lax.broadcasted_iota(jnp.int32, (count, final.shape[2]), 1)
    half = final.shape[2] // 2
    tok = jnp.broadcast_to(tok_ref[...].astype(jnp.float32), (packed_lanes, count)).T[:, :packed]
    tok = tok.astype(jnp.int32)
    low = jnp.zeros((count, final.shape[2]), jnp.float32)
    high = low
    for owner in range(n):
        table = final[owner]
        at_low = jnp.where(tok == device + owner * 2 * packed, 1.0, 0.0).astype(jnp.bfloat16)
        at_high = jnp.where(tok == device + (owner * 2 + 1) * packed, 1.0, 0.0).astype(jnp.bfloat16)
        low = low + jnp.dot(at_low, table, preferred_element_type=jnp.float32)
        high = high + jnp.dot(at_high, table, preferred_element_type=jnp.float32)
    ordered_ref[...] = jnp.where(lane < half, low, high).astype(jnp.bfloat16)


def modulate_kernel(ordered_ref, embed_ref, shift_ref, scale_ref, out_ref):
    embed = embed_ref[...]
    both = jnp.concatenate([embed, embed], axis=0)
    embedded = jnp.dot(ordered_ref[...], both, preferred_element_type=jnp.float32)
    inverse = 1.0 / embedded.shape[1]
    center = jnp.sum(embedded, axis=-1, keepdims=True) * inverse
    centered = embedded - center
    variance = jnp.sum(centered * centered, axis=-1, keepdims=True) * inverse
    normed = centered * lax.rsqrt(variance + EPS)
    out_ref[...] = (normed * (1.0 + scale_ref[...]) + shift_ref[...]).astype(jnp.bfloat16)


def prepare(weight, lanes, rows):
    channels, outs = weight.shape[1], weight.shape[2]
    split = weight.reshape(3, 3, 3, channels, outs).transpose(4, 1, 0, 2, 3)
    split = split.reshape(outs, 3, 9 * channels)
    padded = jnp.pad(split, ((0, rows - outs), (0, 0), (0, lanes - 9 * channels)))
    return padded.reshape(rows, 3 * lanes)


def body(
    n, pairs,
    features, clip_ids, gain_first, weight_first, gain_second, weight_second, gain_third,
    weight_out, embed_weight, shift_mod, scale_mod, token_order,
):
    frames, height, breadth, channels = features.shape
    per, latents = weight_first.shape[2], weight_out.shape[2]
    size = height * breadth
    lanes = -(-9 * channels // 256) * 256
    count = token_order.shape[0]
    width = embed_weight.shape[1]
    patches = frames * size // 4
    packed = patches // 2

    split = per == 12
    rows = 8 if split else -(-per // 8) * 8
    whole_rows = 16 if split else rows
    wide = lanes + lanes // 2 if split else lanes
    place = np.zeros((n * whole_rows, channels), np.float32)
    for channel in range(channels):
        owner, row = divmod(channel, per)
        place[(row // rows * n + owner) * rows + row % rows, channel] = 1
    f, i, j = np.meshgrid(np.arange(frames), np.arange(height), np.arange(breadth), indexing="ij")
    patch = ((f * (height // 2) + i // 2) * (breadth // 2) + j // 2).reshape(-1)
    quarter = (2 * (i % 2) + j % 2).reshape(-1)
    pool = (patch[None, :] % packed == np.arange(packed)[:, None]).astype(np.float32)
    group = np.arange(8 * latents) // latents
    keep = (group[None, :] == (patch // packed * 4 + quarter)[:, None]).astype(np.float32)

    chips = n // 2
    hops = max(1, chips // 2)
    vmem = pl.BlockSpec(memory_space=pltpu.VMEM)
    dma = pltpu.SemaphoreType.DMA
    ordered = pl.pallas_call(
        functools.partial(block_kernel, n, pairs, per, frames, height, breadth),
        out_shape=jax.ShapeDtypeStruct((count, 8 * latents), jnp.bfloat16),
        in_specs=[pl.BlockSpec(memory_space=pltpu.SMEM)] + [vmem] * 11,
        out_specs=vmem,
        scratch_shapes=[
            pltpu.VMEM((2, n, 3, rows, wide), jnp.bfloat16),
            pltpu.VMEM((3, frames, size * 3 // 2, 128), jnp.bfloat16),
            pltpu.VMEM((3, frames, size * 3 // 2, 128), jnp.bfloat16),
            pltpu.VMEM((frames, size, lanes), jnp.bfloat16),
            pltpu.VMEM((frames * size, 8 * latents), jnp.bfloat16),
            pltpu.VMEM((packed, 8 * latents), jnp.bfloat16),
            pltpu.VMEM((n, packed, 8 * latents), jnp.bfloat16),
            dma((2, 3, 2, hops)), dma((2, 3, 2, hops)),
            dma((2, 2, hops)), dma((2, 2, hops)),
            dma((2, 1 + 6 * hops)), dma((2, 1 + 6 * hops)),
            dma((1,)), dma((3, frames)), dma((3, frames)),
            dma((chips,)), dma((chips,)), dma((chips,)), dma((chips,)),
        ],
        compiler_params=pltpu.CompilerParams(
            collective_id=0, has_side_effects=True, vmem_limit_bytes=60 * 1024 * 1024
        ),
        name="block",
    )(
        clip_ids, features.reshape(frames * size, channels),
        gain_first.reshape(1, channels), gain_second.reshape(1, channels),
        gain_third.reshape(1, channels),
        prepare(weight_first, lanes, whole_rows), prepare(weight_second, lanes, whole_rows),
        prepare(weight_out, lanes, latents),
        jnp.asarray(place, jnp.bfloat16), token_order.reshape(1, count),
        jnp.asarray(pool, jnp.bfloat16), jnp.asarray(keep, jnp.bfloat16),
    )
    tile = count // 4
    return pl.pallas_call(
        modulate_kernel,
        out_shape=jax.ShapeDtypeStruct((count, width), jnp.bfloat16),
        grid=(count // tile,),
        in_specs=[
            pl.BlockSpec((tile, 8 * latents), lambda step: (step, 0)),
            pl.BlockSpec((embed_weight.shape[0], width), lambda step: (0, 0)),
            pl.BlockSpec((1, width), lambda step: (0, 0)),
            pl.BlockSpec((1, width), lambda step: (0, 0)),
        ],
        out_specs=pl.BlockSpec((tile, width), lambda step: (step, 0)),
        name="modulate",
    )(ordered, embed_weight, shift_mod.reshape(1, width), scale_mod.reshape(1, width))


def solution(mesh):
    in_specs = (
        P(("groups", "ctx"), None, None, None),
        P("groups"),
        P(),
        P(None, None, "ctx"),
        P(),
        P(None, None, "ctx"),
        P(),
        P(),
        P(),
        P(),
        P(),
        P(("groups", "ctx")),
    )
    out_specs = P(("groups", "ctx"), None)
    return jax.shard_map(
        functools.partial(body, mesh.shape["ctx"], mesh.shape["groups"] % 2 == 0),
        mesh=mesh, in_specs=in_specs, out_specs=out_specs, check_vma=False,
    )
```

```python
import functools

import jax
import jax.numpy as jnp
import numpy as np
from jax import lax
from jax.experimental import pallas as pl
from jax.experimental.pallas import tpu as pltpu
from jax.sharding import PartitionSpec as P

MESH = pl.DeviceIdType.MESH
EPS = 1e-06


def ring_chip(place, chips):
    half = chips // 2
    return jnp.where(place < half, 2 * place, 2 * (chips - 1 - place) + 1)


def ring_place(chip, chips):
    return jnp.where(chip % 2 == 0, chip // 2, chips - 1 - chip // 2)


def rms_silu(values, gain):
    mean = jnp.sum(values * values, axis=-1, keepdims=True) * (1.0 / values.shape[-1])
    normed = values * lax.rsqrt(mean + EPS) * gain
    return (normed / (1.0 + jnp.exp(-normed))).astype(jnp.bfloat16)


def nt_dot(left, right):
    return lax.dot_general(left, right, (((1,), (1,)), ((), ())), preferred_element_type=jnp.float32)


def block_kernel(
    n, pairs, per, frames, height, breadth,
    clip_ref, features_ref, gain1_ref, gain2_ref, gain3_ref, own1_ref, own2_ref, raw_out_ref,
    place_ref, tok_ref, pool_ref, keep_ref,
    ordered_ref,
    gathered, halo, acts, taps, latent, patches, final,
    ring_send, ring_recv, cross_send, cross_recv, pair_send, pair_recv, local_sem,
    halo_send, halo_recv, patch_send, patch_recv, fwd_send, fwd_recv, out_w_ref,
):
    me = lax.axis_index("ctx")
    group = lax.axis_index("groups")
    core, chip = lax.rem(me, 2), lax.div(me, 2)
    parity = lax.rem(group, 2)
    chips = n // 2
    place = ring_place(chip, chips)
    partner = me + 1 - 2 * core
    follower = lax.rem(me + 1, n)
    size = height * breadth
    channels = features_ref.shape[1]
    depth = 9 * channels
    lanes = taps.shape[2]
    rows = gathered.shape[3]
    split = gathered.shape[4] > lanes

    def at(offset):
        return ring_chip(lax.rem(place + offset + chips, chips), chips) * 2 + core

    def rows_of(frame):
        return slice(frame * size, (frame + 1) * size)

    def pack(values, which, frame):
        over = values[:, 128:]
        acts[which, frame, :size, :] = values[:, :128].astype(jnp.bfloat16)
        both = jnp.concatenate([over[: size // 2], over[size // 2 :]], axis=1)
        acts[which, frame, size:, :] = both.astype(jnp.bfloat16)

    def unpack(which, frame):
        both = halo[which, frame, size:, :].astype(jnp.float32)
        over = jnp.concatenate([both[:, : channels - 128], both[:, channels - 128 :]], axis=0)
        return jnp.concatenate([halo[which, frame, :size, :].astype(jnp.float32), over], axis=1)

    def place_own(w, part, values):
        if split:
            rest = values.astype(jnp.float32)[rows:]
            rest = rest[:, : lanes // 2] + pltpu.roll(rest[:, lanes // 2 :], rows // 2, 0)
            gathered[w, me, part, :, lanes:] = rest.astype(jnp.bfloat16)
        gathered[w, me, part, :, :lanes] = values[:rows]

    for part in range(3):
        for w, own in enumerate((own1_ref, own2_ref)):
            place_own(w, part, own[:, part * lanes : (part + 1) * lanes])
    for frame in range(frames):
        pack(features_ref[rows_of(frame), :].astype(jnp.float32), 0, frame)

    barrier = pltpu.get_barrier_semaphore()
    for step in range(1, n):
        pl.semaphore_signal(
            barrier, inc=1, device_id={"ctx": lax.rem(me + step, n)}, device_id_type=MESH
        )
    if pairs:
        peer = group + 1 - 2 * parity
        pl.semaphore_signal(barrier, inc=1, device_id={"groups": peer}, device_id_type=MESH)
    pl.semaphore_wait(barrier, n if pairs else n - 1)

    half_way = chips // 2
    if pairs:
        ring_parts = (0, 1 + parity)
        cross_part = 2 - parity
        reach = ((half_way, chips - 1 - half_way), (chips - 1 - half_way, half_way))
    else:
        ring_parts = (0, 1, 2)
        reach = ((half_way, chips - 1 - half_way),) * 3
    hops = ring_send.shape[3]
    last = len(ring_parts) - 1

    def origin_of(way, step):
        return at(-step - 1) if way == 0 else at(step + 1)

    def ring_copy(w, k, way, step):
        block = gathered.at[w, me if step == 0 else origin_of(way, step - 1), ring_parts[k]]
        return pltpu.make_async_remote_copy(
            src_ref=block, dst_ref=block,
            send_sem=ring_send.at[w, k, way, step], recv_sem=ring_recv.at[w, k, way, step],
            device_id={"ctx": at(1) if way == 0 else at(-1)}, device_id_type=MESH,
        )

    def cross_copy(w, way, step, part):
        block = gathered.at[w, origin_of(way, step), part]
        return pltpu.make_async_remote_copy(
            src_ref=block, dst_ref=block,
            send_sem=cross_send.at[w, way, step], recv_sem=cross_recv.at[w, way, step],
            device_id={"groups": peer}, device_id_type=MESH,
        )

    def own_pair(w):
        block = gathered.at[w, me]
        return pltpu.make_async_remote_copy(
            src_ref=block, dst_ref=block,
            send_sem=pair_send.at[w, 0], recv_sem=pair_recv.at[w, 0],
            device_id={"ctx": partner}, device_id_type=MESH,
        )

    def pair_copy(w, k, way, step):
        part = ring_parts[k] if k <= last else cross_part
        block = gathered.at[w, origin_of(way, step), part]
        slot = 1 + (k * 2 + way) * hops + step
        return pltpu.make_async_remote_copy(
            src_ref=block, dst_ref=block,
            send_sem=pair_send.at[w, slot], recv_sem=pair_recv.at[w, slot],
            device_id={"ctx": partner}, device_id_type=MESH,
        )

    def begin(w):
        for k in range(last, -1, -1):
            for way in range(2):
                if reach[k][way] > 0:
                    ring_copy(w, k, way, 0).start()
        own_pair(w).start()

    def arrive(w, step):
        if pairs and step >= 0:
            for way in range(2):
                if step < reach[last][way]:
                    cross_copy(w, way, step, cross_part).wait_recv()
                    pair_copy(w, last + 1, way, step).start()

    def advance(w, step):
        for k in range(last, -1, -1):
            for way in range(2):
                if step < reach[k][way]:
                    ring_copy(w, k, way, step).wait_recv()
                    if step + 1 < reach[k][way]:
                        ring_copy(w, k, way, step + 1).start()
                    if pairs and k == last:
                        cross_copy(w, way, step, ring_parts[k]).start()
                    pair_copy(w, k, way, step).start()
        arrive(w, step - 1)

    def finish(w):
        arrive(w, half_way - 1)
        own_pair(w).wait()
        for k in range(last + 1):
            for way in range(2):
                for step in range(reach[k][way]):
                    ring_copy(w, k, way, step).wait_send()
                    if pairs and k == last:
                        cross_copy(w, way, step, ring_parts[k]).wait_send()
                        pair_copy(w, k + 1, way, step).wait()
                    pair_copy(w, k, way, step).wait()

    def halo_copy(which, frame):
        return pltpu.make_async_remote_copy(
            src_ref=acts.at[which, frame], dst_ref=halo.at[which, frame],
            send_sem=halo_send.at[which, frame], recv_sem=halo_recv.at[which, frame],
            device_id={"ctx": follower}, device_id_type=MESH,
        )

    begin(0)
    for frame in range(frames):
        halo_copy(0, frame).start()

    def kept(tap, frame):
        position = me * frames + frame - 2 + tap
        seen = clip_ref[jnp.maximum(position, 0)]
        same = jnp.logical_and(position >= 0, seen == clip_ref[me * frames + frame])
        return jnp.where(same, 1.0, 0.0)

    columns = lax.broadcasted_iota(jnp.int32, (height, breadth, channels), 1).reshape(size, channels)

    def lay(values, frame_in):
        wide = values.astype(jnp.float32)
        shifted = (
            jnp.where(columns == 0, 0.0, pltpu.roll(wide, 1, 0)),
            wide,
            jnp.where(columns == breadth - 1, 0.0, pltpu.roll(wide, size - 1, 0)),
        )
        for col_tap in range(3):
            for frame in range(frames):
                tap = frame_in - frame
                if 0 <= tap <= 2:
                    piece = shifted[col_tap]
                    if tap < 2:
                        piece = piece * kept(tap, frame)
                    start = (tap * 3 + col_tap) * channels
                    taps[frame, :, start : start + channels] = piece.astype(jnp.bfloat16)

    for frame in range(frames):
        taps[frame, :, depth:] = jnp.zeros((size, lanes - depth), jnp.bfloat16)

    def spread(parts):
        up, mid, down = parts
        zero = jnp.zeros((breadth, mid.shape[1]), jnp.float32)
        return (
            mid
            + jnp.concatenate([zero, up[: size - breadth]], axis=0)
            + jnp.concatenate([down[breadth:], zero], axis=0)
        )

    def conv(frame, w):
        if not split:
            left = taps[frame]
            return spread([
                nt_dot(left, gathered[w, :, part].reshape(n * rows, lanes)) for part in range(3)
            ])
        halves = []
        for half in range(2):
            span = slice(half * lanes // 2, (half + 1) * lanes // 2)
            left = taps[frame, :, span]
            sums = []
            for part in range(3):
                main = gathered[w, :, part, :, span].reshape(n * rows, lanes // 2)
                rest = gathered[w, :, part, :, lanes:].reshape(n * rows, lanes // 2)
                sums.append(nt_dot(left, jnp.concatenate([main, rest], axis=0)))
            halves.append(spread(sums))
        own, other = halves
        edge = n * rows
        moved = pltpu.roll(other[:, edge:], edge - rows // 2, 1)
        return jnp.concatenate([own[:, :edge] + other[:, :edge], own[:, edge:] + moved], axis=1)

    def out_weight(row_tap):
        part = out_w_ref[:, row_tap * lanes : (row_tap + 1) * lanes]
        return jnp.concatenate([part] * 8, axis=0)

    def compact(values):
        return jnp.dot(values, place_ref[...], preferred_element_type=jnp.float32)

    gain1, gain2, gain3 = gain1_ref[...], gain2_ref[...], gain3_ref[...]

    for part in range(3):
        for tap in range(9):
            start = part * lanes + tap * channels
            out_w_ref[:, start : start + channels] = raw_out_ref[tap // 3 * 9 + part * 3 + tap % 3]
        out_w_ref[:, part * lanes + depth : (part + 1) * lanes] = jnp.zeros(
            (out_w_ref.shape[0], lanes - depth), jnp.bfloat16
        )
    for frame in range(frames):
        lay(rms_silu(features_ref[rows_of(frame), :].astype(jnp.float32), gain1), 2 + frame)
    advance(0, 0)
    for frame in range(frames):
        halo_copy(0, frame).wait()
        lay(rms_silu(unpack(0, frame), gain1), frame)
    for step in range(1, half_way):
        if step == 1:
            begin(1)
        advance(0, step)
        if step >= 2:
            advance(1, step - 2)
    if half_way < 2:
        begin(1)
    finish(0)

    own = []
    for frame in range(frames):
        first = compact(conv(frame, 0).astype(jnp.bfloat16))
        value = rms_silu(first, gain2)
        pack(value.astype(jnp.float32), 1, frame)
        halo_copy(1, frame).start()
        if max(0, half_way - 2) + frame < half_way:
            advance(1, max(0, half_way - 2) + frame)
        own.append(value)
    for frame in range(frames):
        lay(own[frame], 2 + frame)
    for step in range(max(0, half_way - 2) + frames, half_way):
        advance(1, step)
    for frame in range(frames):
        halo_copy(1, frame).wait()
        lay(unpack(1, frame), frame)
    finish(1)

    own = []
    for frame in range(frames):
        base = nt_dot(features_ref[rows_of(frame), :], place_ref[...])
        block = compact((base + conv(frame, 1)).astype(jnp.bfloat16))
        value = rms_silu(block, gain3)
        pack(value.astype(jnp.float32), 2, frame)
        halo_copy(2, frame).start()
        own.append(value)
    for frame in range(frames):
        lay(own[frame], 2 + frame)
    for frame in range(frames):
        halo_copy(2, frame).wait()
        lay(unpack(2, frame), frame)
    for frame in range(frames):
        left = taps[frame]
        sums = spread([nt_dot(left, out_weight(part)) for part in range(3)])
        latent[rows_of(frame), :] = sums.astype(jnp.bfloat16) * keep_ref[rows_of(frame), :]
    patches[...] = jnp.dot(
        pool_ref[...], latent[...], preferred_element_type=jnp.float32
    ).astype(jnp.bfloat16)

    def patch_copy(step):
        return pltpu.make_async_remote_copy(
            src_ref=patches, dst_ref=final.at[me],
            send_sem=patch_send.at[step], recv_sem=patch_recv.at[step],
            device_id={"ctx": lax.rem(me + 2 * step, n)}, device_id_type=MESH,
        )

    def forward_copy(step):
        origin = lax.rem(me + n - 2 * step, n)
        return pltpu.make_async_remote_copy(
            src_ref=patches if step == 0 else final.at[origin], dst_ref=final.at[origin],
            send_sem=fwd_send.at[step], recv_sem=fwd_recv.at[step],
            device_id={"ctx": partner}, device_id_type=MESH,
        )

    order = sorted(range(1, chips), key=lambda step: min(step, chips - step))
    for step in reversed(order):
        patch_copy(step).start()
    forward_copy(0).start()
    mine = pltpu.make_async_copy(patches, final.at[me], local_sem.at[0])
    mine.start()
    for step in order:
        patch_copy(step).wait_recv()
        forward_copy(step).start()
    mine.wait()
    for step in order:
        patch_copy(step).wait_send()
    for step in range(chips):
        forward_copy(step).wait()

    packed, packed_lanes = final.shape[1], final.shape[2]
    count = tok_ref.shape[1]
    device = lax.broadcasted_iota(jnp.int32, (count, packed), 1)
    lane = lax.broadcasted_iota(jnp.int32, (count, final.shape[2]), 1)
    half = final.shape[2] // 2
    tok = jnp.broadcast_to(tok_ref[...].astype(jnp.float32), (packed_lanes, count)).T[:, :packed]
    tok = tok.astype(jnp.int32)
    low = jnp.zeros((count, final.shape[2]), jnp.float32)
    high = low
    for owner in range(n):
        table = final[owner]
        at_low = jnp.where(tok == device + owner * 2 * packed, 1.0, 0.0).astype(jnp.bfloat16)
        at_high = jnp.where(tok == device + (owner * 2 + 1) * packed, 1.0, 0.0).astype(jnp.bfloat16)
        low = low + jnp.dot(at_low, table, preferred_element_type=jnp.float32)
        high = high + jnp.dot(at_high, table, preferred_element_type=jnp.float32)
    ordered_ref[...] = jnp.where(lane < half, low, high).astype(jnp.bfloat16)


def modulate_kernel(ordered_ref, embed_ref, shift_ref, scale_ref, out_ref):
    embed = embed_ref[...]
    both = jnp.concatenate([embed, embed], axis=0)
    embedded = jnp.dot(ordered_ref[...], both, preferred_element_type=jnp.float32)
    inverse = 1.0 / embedded.shape[1]
    center = jnp.sum(embedded, axis=-1, keepdims=True) * inverse
    centered = embedded - center
    variance = jnp.sum(centered * centered, axis=-1, keepdims=True) * inverse
    normed = centered * lax.rsqrt(variance + EPS)
    out_ref[...] = (normed * (1.0 + scale_ref[...]) + shift_ref[...]).astype(jnp.bfloat16)


def prepare(weight, lanes, rows):
    channels, outs = weight.shape[1], weight.shape[2]
    split = weight.reshape(3, 3, 3, channels, outs).transpose(4, 1, 0, 2, 3)
    split = split.reshape(outs, 3, 9 * channels)
    padded = jnp.pad(split, ((0, rows - outs), (0, 0), (0, lanes - 9 * channels)))
    return padded.reshape(rows, 3 * lanes)


def body(
    n, pairs,
    features, clip_ids, gain_first, weight_first, gain_second, weight_second, gain_third,
    weight_out, embed_weight, shift_mod, scale_mod, token_order,
):
    frames, height, breadth, channels = features.shape
    per, latents = weight_first.shape[2], weight_out.shape[2]
    size = height * breadth
    lanes = -(-9 * channels // 256) * 256
    count = token_order.shape[0]
    width = embed_weight.shape[1]
    patches = frames * size // 4
    packed = patches // 2

    split = per == 12
    rows = 8 if split else -(-per // 8) * 8
    whole_rows = 16 if split else rows
    wide = lanes + lanes // 2 if split else lanes
    place = np.zeros((n * whole_rows, channels), np.float32)
    for channel in range(channels):
        owner, row = divmod(channel, per)
        place[(row // rows * n + owner) * rows + row % rows, channel] = 1
    f, i, j = np.meshgrid(np.arange(frames), np.arange(height), np.arange(breadth), indexing="ij")
    patch = ((f * (height // 2) + i // 2) * (breadth // 2) + j // 2).reshape(-1)
    quarter = (2 * (i % 2) + j % 2).reshape(-1)
    pool = (patch[None, :] % packed == np.arange(packed)[:, None]).astype(np.float32)
    group = np.arange(8 * latents) // latents
    keep = (group[None, :] == (patch // packed * 4 + quarter)[:, None]).astype(np.float32)

    chips = n // 2
    hops = max(1, chips // 2)
    vmem = pl.BlockSpec(memory_space=pltpu.VMEM)
    dma = pltpu.SemaphoreType.DMA
    ordered = pl.pallas_call(
        functools.partial(block_kernel, n, pairs, per, frames, height, breadth),
        out_shape=jax.ShapeDtypeStruct((count, 8 * latents), jnp.bfloat16),
        in_specs=[pl.BlockSpec(memory_space=pltpu.SMEM)] + [vmem] * 11,
        out_specs=vmem,
        scratch_shapes=[
            pltpu.VMEM((2, n, 3, rows, wide), jnp.bfloat16),
            pltpu.VMEM((3, frames, size * 3 // 2, 128), jnp.bfloat16),
            pltpu.VMEM((3, frames, size * 3 // 2, 128), jnp.bfloat16),
            pltpu.VMEM((frames, size, lanes), jnp.bfloat16),
            pltpu.VMEM((frames * size, 8 * latents), jnp.bfloat16),
            pltpu.VMEM((packed, 8 * latents), jnp.bfloat16),
            pltpu.VMEM((n, packed, 8 * latents), jnp.bfloat16),
            dma((2, 3, 2, hops)), dma((2, 3, 2, hops)),
            dma((2, 2, hops)), dma((2, 2, hops)),
            dma((2, 1 + 6 * hops)), dma((2, 1 + 6 * hops)),
            dma((1,)), dma((3, frames)), dma((3, frames)),
            dma((chips,)), dma((chips,)), dma((chips,)), dma((chips,)),
            pltpu.VMEM((latents, 3 * lanes), jnp.bfloat16),
        ],
        compiler_params=pltpu.CompilerParams(
            collective_id=0, has_side_effects=True, vmem_limit_bytes=60 * 1024 * 1024
        ),
        name="block",
    )(
        clip_ids, features.reshape(frames * size, channels),
        gain_first.reshape(1, channels), gain_second.reshape(1, channels),
        gain_third.reshape(1, channels),
        prepare(weight_first, lanes, whole_rows), prepare(weight_second, lanes, whole_rows),
        weight_out.transpose(0, 2, 1),
        jnp.asarray(place, jnp.bfloat16), token_order.reshape(1, count),
        jnp.asarray(pool, jnp.bfloat16), jnp.asarray(keep, jnp.bfloat16),
    )
    tile = count // 4
    return pl.pallas_call(
        modulate_kernel,
        out_shape=jax.ShapeDtypeStruct((count, width), jnp.bfloat16),
        grid=(count // tile,),
        in_specs=[
            pl.BlockSpec((tile, 8 * latents), lambda step: (step, 0)),
            pl.BlockSpec((embed_weight.shape[0], width), lambda step: (0, 0)),
            pl.BlockSpec((1, width), lambda step: (0, 0)),
            pl.BlockSpec((1, width), lambda step: (0, 0)),
        ],
        out_specs=pl.BlockSpec((tile, width), lambda step: (step, 0)),
        name="modulate",
    )(ordered, embed_weight, shift_mod.reshape(1, width), scale_mod.reshape(1, width))


def solution(mesh):
    in_specs = (
        P(("groups", "ctx"), None, None, None),
        P("groups"),
        P(),
        P(None, None, "ctx"),
        P(),
        P(None, None, "ctx"),
        P(),
        P(),
        P(),
        P(),
        P(),
        P(("groups", "ctx")),
    )
    out_specs = P(("groups", "ctx"), None)
    return jax.shard_map(
        functools.partial(body, mesh.shape["ctx"], mesh.shape["groups"] % 2 == 0),
        mesh=mesh, in_specs=in_specs, out_specs=out_specs, check_vma=False,
    )
```

```python
import functools

import jax
import jax.numpy as jnp
import numpy as np
from jax import lax
from jax.experimental import pallas as pl
from jax.experimental.pallas import tpu as pltpu
from jax.sharding import PartitionSpec as P

MESH = pl.DeviceIdType.MESH
EPS = 1e-06


def ring_chip(place, chips):
    half = chips // 2
    return jnp.where(place < half, 2 * place, 2 * (chips - 1 - place) + 1)


def ring_place(chip, chips):
    return jnp.where(chip % 2 == 0, chip // 2, chips - 1 - chip // 2)


def rms_silu(values, gain):
    mean = jnp.sum(values * values, axis=-1, keepdims=True) * (1.0 / values.shape[-1])
    normed = values * lax.rsqrt(mean + EPS) * gain
    return (normed / (1.0 + jnp.exp(-normed))).astype(jnp.bfloat16)


def nt_dot(left, right):
    return lax.dot_general(left, right, (((1,), (1,)), ((), ())), preferred_element_type=jnp.float32)


def block_kernel(
    n, pairs, per, frames, height, breadth,
    clip_ref, features_ref, gain1_ref, gain2_ref, gain3_ref, own1_ref, own2_ref, raw_out_ref,
    place_ref, tok_ref, pool_ref, keep_ref,
    ordered_ref,
    gathered, halo, acts, taps, latent, patches, final,
    ring_send, ring_recv, cross_send, cross_recv, pair_send, pair_recv, local_sem,
    halo_send, halo_recv, patch_send, patch_recv, fwd_send, fwd_recv, out_w_ref, own_ref,
):
    me = lax.axis_index("ctx")
    group = lax.axis_index("groups")
    core, chip = lax.rem(me, 2), lax.div(me, 2)
    parity = lax.rem(group, 2)
    chips = n // 2
    place = ring_place(chip, chips)
    partner = me + 1 - 2 * core
    follower = lax.rem(me + 1, n)
    size = height * breadth
    channels = features_ref.shape[1]
    depth = 9 * channels
    lanes = taps.shape[2]
    rows = gathered.shape[3]
    split = gathered.shape[4] > lanes

    def at(offset):
        return ring_chip(lax.rem(place + offset + chips, chips), chips) * 2 + core

    def rows_of(frame):
        return slice(frame * size, (frame + 1) * size)

    def pack(values, which, frame):
        over = values[:, 128:]
        acts[which, frame, :size, :] = values[:, :128].astype(jnp.bfloat16)
        both = jnp.concatenate([over[: size // 2], over[size // 2 :]], axis=1)
        acts[which, frame, size:, :] = both.astype(jnp.bfloat16)

    def unpack(which, frame):
        both = halo[which, frame, size:, :].astype(jnp.float32)
        over = jnp.concatenate([both[:, : channels - 128], both[:, channels - 128 :]], axis=0)
        return jnp.concatenate([halo[which, frame, :size, :].astype(jnp.float32), over], axis=1)

    def place_own(w, part, values):
        if split:
            rest = values.astype(jnp.float32)[rows:]
            rest = rest[:, : lanes // 2] + pltpu.roll(rest[:, lanes // 2 :], rows // 2, 0)
            gathered[w, me, part, :, lanes:] = rest.astype(jnp.bfloat16)
        gathered[w, me, part, :, :lanes] = values[:rows]

    def lay_own(w, raw):
        own_ref[w] = jnp.zeros(own_ref.shape[1:], jnp.bfloat16)
        for part in range(3):
            for tap in range(9):
                start = part * lanes + tap * channels
                own_ref[w, :per, start : start + channels] = raw[:, tap // 3 * 9 + part * 3 + tap % 3, :]
            place_own(w, part, own_ref[w, :, part * lanes : (part + 1) * lanes])

    lay_own(0, own1_ref)
    for frame in range(frames):
        pack(features_ref[rows_of(frame), :].astype(jnp.float32), 0, frame)

    barrier = pltpu.get_barrier_semaphore()
    for step in range(1, n):
        pl.semaphore_signal(
            barrier, inc=1, device_id={"ctx": lax.rem(me + step, n)}, device_id_type=MESH
        )
    if pairs:
        peer = group + 1 - 2 * parity
        pl.semaphore_signal(barrier, inc=1, device_id={"groups": peer}, device_id_type=MESH)
    pl.semaphore_wait(barrier, n if pairs else n - 1)

    half_way = chips // 2
    if pairs:
        ring_parts = (0, 1 + parity)
        cross_part = 2 - parity
        reach = ((half_way, chips - 1 - half_way), (chips - 1 - half_way, half_way))
    else:
        ring_parts = (0, 1, 2)
        reach = ((half_way, chips - 1 - half_way),) * 3
    hops = ring_send.shape[3]
    last = len(ring_parts) - 1

    def origin_of(way, step):
        return at(-step - 1) if way == 0 else at(step + 1)

    def ring_copy(w, k, way, step):
        block = gathered.at[w, me if step == 0 else origin_of(way, step - 1), ring_parts[k]]
        return pltpu.make_async_remote_copy(
            src_ref=block, dst_ref=block,
            send_sem=ring_send.at[w, k, way, step], recv_sem=ring_recv.at[w, k, way, step],
            device_id={"ctx": at(1) if way == 0 else at(-1)}, device_id_type=MESH,
        )

    def cross_copy(w, way, step, part):
        block = gathered.at[w, origin_of(way, step), part]
        return pltpu.make_async_remote_copy(
            src_ref=block, dst_ref=block,
            send_sem=cross_send.at[w, way, step], recv_sem=cross_recv.at[w, way, step],
            device_id={"groups": peer}, device_id_type=MESH,
        )

    def own_pair(w):
        block = gathered.at[w, me]
        return pltpu.make_async_remote_copy(
            src_ref=block, dst_ref=block,
            send_sem=pair_send.at[w, 0], recv_sem=pair_recv.at[w, 0],
            device_id={"ctx": partner}, device_id_type=MESH,
        )

    def pair_copy(w, k, way, step):
        part = ring_parts[k] if k <= last else cross_part
        block = gathered.at[w, origin_of(way, step), part]
        slot = 1 + (k * 2 + way) * hops + step
        return pltpu.make_async_remote_copy(
            src_ref=block, dst_ref=block,
            send_sem=pair_send.at[w, slot], recv_sem=pair_recv.at[w, slot],
            device_id={"ctx": partner}, device_id_type=MESH,
        )

    def begin(w):
        for k in range(last, -1, -1):
            for way in range(2):
                if reach[k][way] > 0:
                    ring_copy(w, k, way, 0).start()
        own_pair(w).start()

    def arrive(w, step):
        if pairs and step >= 0:
            for way in range(2):
                if step < reach[last][way]:
                    cross_copy(w, way, step, cross_part).wait_recv()
                    pair_copy(w, last + 1, way, step).start()

    def advance(w, step):
        for k in range(last, -1, -1):
            for way in range(2):
                if step < reach[k][way]:
                    ring_copy(w, k, way, step).wait_recv()
                    if step + 1 < reach[k][way]:
                        ring_copy(w, k, way, step + 1).start()
                    if pairs and k == last:
                        cross_copy(w, way, step, ring_parts[k]).start()
                    pair_copy(w, k, way, step).start()
        arrive(w, step - 1)

    def finish(w):
        arrive(w, half_way - 1)
        own_pair(w).wait()
        for k in range(last + 1):
            for way in range(2):
                for step in range(reach[k][way]):
                    ring_copy(w, k, way, step).wait_send()
                    if pairs and k == last:
                        cross_copy(w, way, step, ring_parts[k]).wait_send()
                        pair_copy(w, k + 1, way, step).wait()
                    pair_copy(w, k, way, step).wait()

    def halo_copy(which, frame):
        return pltpu.make_async_remote_copy(
            src_ref=acts.at[which, frame], dst_ref=halo.at[which, frame],
            send_sem=halo_send.at[which, frame], recv_sem=halo_recv.at[which, frame],
            device_id={"ctx": follower}, device_id_type=MESH,
        )

    begin(0)
    for frame in range(frames):
        halo_copy(0, frame).start()

    def kept(tap, frame):
        position = me * frames + frame - 2 + tap
        seen = clip_ref[jnp.maximum(position, 0)]
        same = jnp.logical_and(position >= 0, seen == clip_ref[me * frames + frame])
        return jnp.where(same, 1.0, 0.0)

    columns = lax.broadcasted_iota(jnp.int32, (height, breadth, channels), 1).reshape(size, channels)

    def lay(values, frame_in):
        wide = values.astype(jnp.float32)
        shifted = (
            jnp.where(columns == 0, 0.0, pltpu.roll(wide, 1, 0)),
            wide,
            jnp.where(columns == breadth - 1, 0.0, pltpu.roll(wide, size - 1, 0)),
        )
        for col_tap in range(3):
            for frame in range(frames):
                tap = frame_in - frame
                if 0 <= tap <= 2:
                    piece = shifted[col_tap]
                    if tap < 2:
                        piece = piece * kept(tap, frame)
                    start = (tap * 3 + col_tap) * channels
                    taps[frame, :, start : start + channels] = piece.astype(jnp.bfloat16)

    for frame in range(frames):
        taps[frame, :, depth:] = jnp.zeros((size, lanes - depth), jnp.bfloat16)

    def spread(parts):
        up, mid, down = parts
        zero = jnp.zeros((breadth, mid.shape[1]), jnp.float32)
        return (
            mid
            + jnp.concatenate([zero, up[: size - breadth]], axis=0)
            + jnp.concatenate([down[breadth:], zero], axis=0)
        )

    def conv(frame, w):
        if not split:
            left = taps[frame]
            return spread([
                nt_dot(left, gathered[w, :, part].reshape(n * rows, lanes)) for part in range(3)
            ])
        halves = []
        for half in range(2):
            span = slice(half * lanes // 2, (half + 1) * lanes // 2)
            left = taps[frame, :, span]
            sums = []
            for part in range(3):
                main = gathered[w, :, part, :, span].reshape(n * rows, lanes // 2)
                rest = gathered[w, :, part, :, lanes:].reshape(n * rows, lanes // 2)
                sums.append(nt_dot(left, jnp.concatenate([main, rest], axis=0)))
            halves.append(spread(sums))
        own, other = halves
        edge = n * rows
        moved = pltpu.roll(other[:, edge:], edge - rows // 2, 1)
        return jnp.concatenate([own[:, :edge] + other[:, :edge], own[:, edge:] + moved], axis=1)

    def out_weight(row_tap):
        part = out_w_ref[:, row_tap * lanes : (row_tap + 1) * lanes]
        return jnp.concatenate([part] * 8, axis=0)

    def compact(values):
        return jnp.dot(values, place_ref[...], preferred_element_type=jnp.float32)

    gain1, gain2, gain3 = gain1_ref[...], gain2_ref[...], gain3_ref[...]

    lay_own(1, own2_ref)
    for part in range(3):
        for tap in range(9):
            start = part * lanes + tap * channels
            out_w_ref[:, start : start + channels] = raw_out_ref[tap // 3 * 9 + part * 3 + tap % 3]
        out_w_ref[:, part * lanes + depth : (part + 1) * lanes] = jnp.zeros(
            (out_w_ref.shape[0], lanes - depth), jnp.bfloat16
        )
    for frame in range(frames):
        lay(rms_silu(features_ref[rows_of(frame), :].astype(jnp.float32), gain1), 2 + frame)
    advance(0, 0)
    for frame in range(frames):
        halo_copy(0, frame).wait()
        lay(rms_silu(unpack(0, frame), gain1), frame)
    for step in range(1, half_way):
        if step == 1:
            begin(1)
        advance(0, step)
        if step >= 2:
            advance(1, step - 2)
    if half_way < 2:
        begin(1)
    finish(0)

    own = []
    for frame in range(frames):
        first = compact(conv(frame, 0).astype(jnp.bfloat16))
        value = rms_silu(first, gain2)
        pack(value.astype(jnp.float32), 1, frame)
        halo_copy(1, frame).start()
        if max(0, half_way - 2) + frame < half_way:
            advance(1, max(0, half_way - 2) + frame)
        own.append(value)
    for frame in range(frames):
        lay(own[frame], 2 + frame)
    for step in range(max(0, half_way - 2) + frames, half_way):
        advance(1, step)
    for frame in range(frames):
        halo_copy(1, frame).wait()
        lay(unpack(1, frame), frame)
    finish(1)

    own = []
    for frame in range(frames):
        base = nt_dot(features_ref[rows_of(frame), :], place_ref[...])
        block = compact((base + conv(frame, 1)).astype(jnp.bfloat16))
        value = rms_silu(block, gain3)
        pack(value.astype(jnp.float32), 2, frame)
        halo_copy(2, frame).start()
        own.append(value)
    for frame in range(frames):
        lay(own[frame], 2 + frame)
    for frame in range(frames):
        halo_copy(2, frame).wait()
        lay(unpack(2, frame), frame)
    for frame in range(frames):
        left = taps[frame]
        sums = spread([nt_dot(left, out_weight(part)) for part in range(3)])
        latent[rows_of(frame), :] = sums.astype(jnp.bfloat16) * keep_ref[rows_of(frame), :]
    patches[...] = jnp.dot(
        pool_ref[...], latent[...], preferred_element_type=jnp.float32
    ).astype(jnp.bfloat16)

    def patch_copy(step):
        return pltpu.make_async_remote_copy(
            src_ref=patches, dst_ref=final.at[me],
            send_sem=patch_send.at[step], recv_sem=patch_recv.at[step],
            device_id={"ctx": lax.rem(me + 2 * step, n)}, device_id_type=MESH,
        )

    def forward_copy(step):
        origin = lax.rem(me + n - 2 * step, n)
        return pltpu.make_async_remote_copy(
            src_ref=patches if step == 0 else final.at[origin], dst_ref=final.at[origin],
            send_sem=fwd_send.at[step], recv_sem=fwd_recv.at[step],
            device_id={"ctx": partner}, device_id_type=MESH,
        )

    order = sorted(range(1, chips), key=lambda step: min(step, chips - step))
    for step in reversed(order):
        patch_copy(step).start()
    forward_copy(0).start()
    mine = pltpu.make_async_copy(patches, final.at[me], local_sem.at[0])
    mine.start()
    for step in order:
        patch_copy(step).wait_recv()
        forward_copy(step).start()
    mine.wait()
    for step in order:
        patch_copy(step).wait_send()
    for step in range(chips):
        forward_copy(step).wait()

    packed, packed_lanes = final.shape[1], final.shape[2]
    count = tok_ref.shape[1]
    device = lax.broadcasted_iota(jnp.int32, (count, packed), 1)
    lane = lax.broadcasted_iota(jnp.int32, (count, final.shape[2]), 1)
    half = final.shape[2] // 2
    tok = jnp.broadcast_to(tok_ref[...].astype(jnp.float32), (packed_lanes, count)).T[:, :packed]
    tok = tok.astype(jnp.int32)
    low = jnp.zeros((count, final.shape[2]), jnp.float32)
    high = low
    for owner in range(n):
        table = final[owner]
        at_low = jnp.where(tok == device + owner * 2 * packed, 1.0, 0.0).astype(jnp.bfloat16)
        at_high = jnp.where(tok == device + (owner * 2 + 1) * packed, 1.0, 0.0).astype(jnp.bfloat16)
        low = low + jnp.dot(at_low, table, preferred_element_type=jnp.float32)
        high = high + jnp.dot(at_high, table, preferred_element_type=jnp.float32)
    ordered_ref[...] = jnp.where(lane < half, low, high).astype(jnp.bfloat16)


def modulate_kernel(ordered_ref, embed_ref, shift_ref, scale_ref, out_ref):
    half = embed_ref.shape[0]
    ordered = ordered_ref[:, :half] + ordered_ref[:, half:]
    embedded = jnp.dot(ordered, embed_ref[...], preferred_element_type=jnp.float32)
    inverse = 1.0 / embedded.shape[1]
    center = jnp.sum(embedded, axis=-1, keepdims=True) * inverse
    centered = embedded - center
    variance = jnp.sum(centered * centered, axis=-1, keepdims=True) * inverse
    normed = centered * lax.rsqrt(variance + EPS)
    out_ref[...] = (normed * (1.0 + scale_ref[...]) + shift_ref[...]).astype(jnp.bfloat16)


def prepare(weight, lanes, rows):
    channels, outs = weight.shape[1], weight.shape[2]
    split = weight.reshape(3, 3, 3, channels, outs).transpose(4, 1, 0, 2, 3)
    split = split.reshape(outs, 3, 9 * channels)
    padded = jnp.pad(split, ((0, rows - outs), (0, 0), (0, lanes - 9 * channels)))
    return padded.reshape(rows, 3 * lanes)


def body(
    n, pairs,
    features, clip_ids, gain_first, weight_first, gain_second, weight_second, gain_third,
    weight_out, embed_weight, shift_mod, scale_mod, token_order,
):
    frames, height, breadth, channels = features.shape
    per, latents = weight_first.shape[2], weight_out.shape[2]
    size = height * breadth
    lanes = -(-9 * channels // 256) * 256
    count = token_order.shape[0]
    width = embed_weight.shape[1]
    patches = frames * size // 4
    packed = patches // 2

    split = per == 12
    rows = 8 if split else -(-per // 8) * 8
    whole_rows = 16 if split else rows
    wide = lanes + lanes // 2 if split else lanes
    place = np.zeros((n * whole_rows, channels), np.float32)
    for channel in range(channels):
        owner, row = divmod(channel, per)
        place[(row // rows * n + owner) * rows + row % rows, channel] = 1
    f, i, j = np.meshgrid(np.arange(frames), np.arange(height), np.arange(breadth), indexing="ij")
    patch = ((f * (height // 2) + i // 2) * (breadth // 2) + j // 2).reshape(-1)
    quarter = (2 * (i % 2) + j % 2).reshape(-1)
    pool = (patch[None, :] % packed == np.arange(packed)[:, None]).astype(np.float32)
    group = np.arange(8 * latents) // latents
    keep = (group[None, :] == (patch // packed * 4 + quarter)[:, None]).astype(np.float32)

    chips = n // 2
    hops = max(1, chips // 2)
    vmem = pl.BlockSpec(memory_space=pltpu.VMEM)
    dma = pltpu.SemaphoreType.DMA
    ordered = pl.pallas_call(
        functools.partial(block_kernel, n, pairs, per, frames, height, breadth),
        out_shape=jax.ShapeDtypeStruct((count, 8 * latents), jnp.bfloat16),
        in_specs=[pl.BlockSpec(memory_space=pltpu.SMEM)] + [vmem] * 11,
        out_specs=vmem,
        scratch_shapes=[
            pltpu.VMEM((2, n, 3, rows, wide), jnp.bfloat16),
            pltpu.VMEM((3, frames, size * 3 // 2, 128), jnp.bfloat16),
            pltpu.VMEM((3, frames, size * 3 // 2, 128), jnp.bfloat16),
            pltpu.VMEM((frames, size, lanes), jnp.bfloat16),
            pltpu.VMEM((frames * size, 8 * latents), jnp.bfloat16),
            pltpu.VMEM((packed, 8 * latents), jnp.bfloat16),
            pltpu.VMEM((n, packed, 8 * latents), jnp.bfloat16),
            dma((2, 3, 2, hops)), dma((2, 3, 2, hops)),
            dma((2, 2, hops)), dma((2, 2, hops)),
            dma((2, 1 + 6 * hops)), dma((2, 1 + 6 * hops)),
            dma((1,)), dma((3, frames)), dma((3, frames)),
            dma((chips,)), dma((chips,)), dma((chips,)), dma((chips,)),
            pltpu.VMEM((latents, 3 * lanes), jnp.bfloat16),
            pltpu.VMEM((2, whole_rows, 3 * lanes), jnp.bfloat16),
        ],
        compiler_params=pltpu.CompilerParams(
            collective_id=0, has_side_effects=True, vmem_limit_bytes=60 * 1024 * 1024
        ),
        name="block",
    )(
        clip_ids, features.reshape(frames * size, channels),
        gain_first.reshape(1, channels), gain_second.reshape(1, channels),
        gain_third.reshape(1, channels),
        weight_first.transpose(2, 0, 1), weight_second.transpose(2, 0, 1),
        weight_out.transpose(0, 2, 1),
        jnp.asarray(place, jnp.bfloat16), token_order.reshape(1, count),
        jnp.asarray(pool, jnp.bfloat16), jnp.asarray(keep, jnp.bfloat16),
    )
    tile = count // 4
    return pl.pallas_call(
        modulate_kernel,
        out_shape=jax.ShapeDtypeStruct((count, width), jnp.bfloat16),
        grid=(count // tile,),
        in_specs=[
            pl.BlockSpec((tile, 8 * latents), lambda step: (step, 0)),
            pl.BlockSpec((embed_weight.shape[0], width), lambda step: (0, 0)),
            pl.BlockSpec((1, width), lambda step: (0, 0)),
            pl.BlockSpec((1, width), lambda step: (0, 0)),
        ],
        out_specs=pl.BlockSpec((tile, width), lambda step: (step, 0)),
        name="modulate",
    )(ordered, embed_weight, shift_mod.reshape(1, width), scale_mod.reshape(1, width))


def solution(mesh):
    in_specs = (
        P(("groups", "ctx"), None, None, None),
        P("groups"),
        P(),
        P(None, None, "ctx"),
        P(),
        P(None, None, "ctx"),
        P(),
        P(),
        P(),
        P(),
        P(),
        P(("groups", "ctx")),
    )
    out_specs = P(("groups", "ctx"), None)
    return jax.shard_map(
        functools.partial(body, mesh.shape["ctx"], mesh.shape["groups"] % 2 == 0),
        mesh=mesh, in_specs=in_specs, out_specs=out_specs, check_vma=False,
    )
```
